32 devices in a mesh: ctx: 8 (over z, core), exp: 4 (over y, x).
Axes of the slice: x: 2, y: 2, z: 4, core: 2. Of those that a mesh axis runs over, the one named last changes fastest.
Arguments:
- x_in: bfloat16 [1024, 4096], P('ctx', 'exp'), may hold values from -6 to 6
- z_gate: bfloat16 [1024, 4096], P('ctx', 'exp'), may hold values from -6 to 6
- b_proj: bfloat16 [1024, 128], P('ctx'), may hold values from -0.5 to 0.5
- c_proj: bfloat16 [1024, 128], P('ctx'), may hold values from -0.5 to 0.5
- dt_raw: float32 [64, 1024], P('exp', 'ctx'), may hold values from -4 to 4
- a_log: float32 [64], P('exp'), may hold values from -13 to -2.9
- d_skip: float32 [64], P('exp'), may hold values from 0.5 to 1.5
- out_proj: bfloat16 [4096, 2048], P('exp'), may hold values from -0.09375 to 0.09375
- residual: bfloat16 [1024, 2048], P('ctx'), may hold values from -80 to 80
- norm_gain: float32 [2048], replicated, may hold values from 0.5 to 1.5
- router: bfloat16 [2048, 16], replicated, may hold values from -0.125 to 0.125
- w_gate: bfloat16 [16, 2048, 7168], P(None, 'ctx', 'exp'), may hold values from -0.125 to 0.125
- w_up: bfloat16 [16, 2048, 7168], P(None, 'ctx', 'exp'), may hold values from -0.125 to 0.125
- w_down: bfloat16 [16, 2048, 7168], P(None, 'ctx', 'exp'), may hold values from -0.0625 to 0.0625
- block_experts: int32 [8, 2], replicated, may hold values from 0 to 15, all different within a row
Outputs:
- stream_out: bfloat16 [1024, 2048], P('ctx', 'exp')
- expert_out: bfloat16 [1024, 2048], P('ctx', 'exp')
The draws below stay inside these ranges and needn't reach their ends.
All inputs are finite; a program needn't handle non-finite values.
Results may differ from the reference program's by a relative error of at most 0.03.
Values may be sent and summed in bfloat16 or wider, within the bound.
No kernel may reach another device: no remote copies, remote signals or barrier semaphores. Data moves between devices by JAX's collectives and lax.ppermute only.
A program may use at most 192 MiB of HBM per device.

```python
import math
import jax
import jax.numpy as jnp
from jax import lax

D = 2048
FF = 7168
EXPERTS = 16
HEADS = 64
HDIM = 64
DSTATE = 128
BLOCK = 128
TOKENS = 1024
INNER = 4096
NBLK = 8
N_EXP = 4


def draw_a_log(key, part):
    first_key, second_key, third_key = jax.random.split(jax.random.fold_in(key, 11), 3)
    slow_share = 0.5
    slow_heads = jax.random.uniform(first_key, (HEADS,)) < slow_share
    fast_rate = 0.03 * jnp.exp(jax.random.uniform(second_key, (HEADS,), minval=-0.5, maxval=0.5))
    slow_rate = jnp.exp(jax.random.uniform(third_key, (HEADS,), minval=math.log(0.2), maxval=math.log(2.0))) / TOKENS
    return jnp.log(jnp.where(slow_heads, slow_rate, fast_rate)).astype(jnp.float32)


def draw_residual(key, part):
    first_key, second_key, third_key = jax.random.split(jax.random.fold_in(key, 23), 3)
    row_scale = jnp.exp(jax.random.uniform(first_key, (TOKENS, 1), minval=0.0, maxval=math.log(10.0)))
    column_place = jnp.arange(D, dtype=jnp.float32)[None, :] / D
    column_scale = jnp.exp(math.log(3.0) * column_place + jax.random.uniform(second_key, (1, D), minval=-0.3, maxval=0.3))
    base_value = jax.random.normal(third_key, (TOKENS, D))
    return (0.3 * base_value * row_scale * column_scale).astype(jnp.bfloat16)


def level_of(rng, extent, cuts, smallest, high):
    factor_of = 1.0
    for dim, blocks in cuts:
        draws = jax.random.uniform(jax.random.fold_in(jax.random.fold_in(rng, 6), dim), (blocks,), jnp.float32, smallest / len(cuts), high / len(cuts))
        factor_of = factor_of * jnp.repeat(jnp.exp(draws), extent[dim] // blocks).reshape((-1,) + (1,) * (len(extent) - 1 - dim))
    return factor_of


def different_ones(key, rows, number_of, top, lift):
    sequence = jax.random.permutation(jax.random.fold_in(key, 1), number_of)
    boost = sequence
    for power in range(3):
        boost = boost * boost // number_of
    boost = boost * lift // number_of
    chance = jax.random.randint(jax.random.fold_in(key, 2), (rows, number_of), 0, 4096) + boost
    fixed_rows = jax.random.permutation(jax.random.fold_in(key, 3), rows)[jnp.arange(number_of) % rows]
    chance = jnp.where(jnp.arange(rows)[:, None] == fixed_rows[None, :], 1 << 14, chance)
    score = chance * number_of + jnp.arange(number_of)
    return lax.top_k(score.astype(jnp.int32), top)[1].astype(jnp.int32)


def centred(own_key, shape, scale, reach, cuts=(), kind=jnp.bfloat16):
    loudness = level_of(own_key, shape, cuts, -0.22, 0.18) if cuts else 1.0
    result = jax.random.normal(own_key, shape, jnp.float32) * scale * loudness
    return jnp.minimum(jnp.maximum(result, -reach), reach).astype(kind)


def setup_inputs(seed: int = 0) -> dict:
    arg_keys = jax.random.split(jax.random.key(seed), 16)
    x_in = centred(arg_keys[0], (TOKENS, INNER), 1.0, 6.0, ((0, 8), (1, 4)))
    z_gate = centred(arg_keys[1], (TOKENS, INNER), 1.0, 6.0, ((0, 8), (1, 4)))
    b_proj = centred(arg_keys[2], (TOKENS, DSTATE), DSTATE ** -0.5, 0.5, ((0, 8),))
    c_proj = centred(arg_keys[3], (TOKENS, DSTATE), DSTATE ** -0.5, 0.5, ((0, 8),))
    dt_raw = centred(arg_keys[4], (HEADS, TOKENS), 1.0, 4.0, ((0, 4), (1, 8)), jnp.float32)
    a_log = draw_a_log(jax.random.fold_in(arg_keys[15], 71), 0)
    d_skip = jnp.clip(1.0 + 0.1 * jax.random.normal(arg_keys[6], (HEADS,), jnp.float32), 0.5, 1.5)
    out_proj = centred(arg_keys[7], (INNER, D), INNER ** -0.5, 0.09375, ((0, 4),))
    residual = draw_residual(jax.random.fold_in(arg_keys[15], 71), 0)
    norm_gain = jnp.clip(1.0 + 0.1 * jax.random.normal(arg_keys[9], (D,), jnp.float32), 0.5, 1.5)
    router = centred(arg_keys[10], (D, EXPERTS), D ** -0.5, 0.125)
    w_gate = centred(arg_keys[11], (EXPERTS, D, FF), D ** -0.5, 0.125, ((1, 8), (2, 4)))
    w_up = centred(arg_keys[12], (EXPERTS, D, FF), D ** -0.5, 0.125, ((1, 8), (2, 4)))
    w_down = centred(arg_keys[13], (EXPERTS, D, FF), FF ** -0.5, 0.0625, ((1, 8), (2, 4)))
    block_experts = different_ones(arg_keys[14], NBLK, EXPERTS, 2, 2048)
    return {"x_in": x_in, "z_gate": z_gate, "b_proj": b_proj, "c_proj": c_proj, "dt_raw": dt_raw, "a_log": a_log, "d_skip": d_skip, "out_proj": out_proj, "residual": residual, "norm_gain": norm_gain, "router": router, "w_gate": w_gate, "w_up": w_up, "w_down": w_down, "block_experts": block_experts}


highest = lax.Precision.HIGHEST
epsilon = 1e-05

def block_terms(inputs_f, steps_f, keys_f, queries_f, head_rates):
    length = inputs_f.shape[0]
    log_decay = -head_rates[:, None] * steps_f
    running = jnp.cumsum(log_decay, axis=1)
    spread = running[:, :, None] - running[:, None, :]
    lower_part = jnp.arange(length)[:, None] >= jnp.arange(length)[None, :]
    weights = jnp.where(lower_part[None], jnp.exp(jnp.minimum(spread, 0.0)), 0.0)
    scores = jnp.dot(queries_f, keys_f.T, precision=highest)
    mixing = scores[None] * weights * steps_f[:, None, :]
    inside = jnp.einsum('hls,shp->lhp', mixing, inputs_f, precision=highest)
    carry_weight = jnp.exp(running[:, -1:] - running) * steps_f
    own_state = jnp.einsum('hs,shp,sn->hpn', carry_weight, inputs_f, keys_f, precision=highest)
    return (inside, own_state, jnp.exp(running), jnp.exp(running[:, -1]))

def reference(x_in, z_gate, b_proj, c_proj, dt_raw, a_log, d_skip, out_proj, residual, norm_gain, router, w_gate, w_up, w_down, block_experts):
    head_rates = jnp.exp(a_log)
    step_sizes = jax.nn.softplus(dt_raw)
    inputs_f = x_in.astype(jnp.float32).reshape(NBLK, BLOCK, HEADS, HDIM)
    steps_f = step_sizes.reshape(HEADS, NBLK, BLOCK).transpose(1, 0, 2)
    keys_f = b_proj.astype(jnp.float32).reshape(NBLK, BLOCK, DSTATE)
    queries_f = c_proj.astype(jnp.float32).reshape(NBLK, BLOCK, DSTATE)

    def advance(carried, pieces):
        inside, own_state, entry_scale, block_decay = block_terms(pieces[0], pieces[1], pieces[2], pieces[3], head_rates)
        from_before = entry_scale.T[:, :, None] * jnp.einsum('ln,hpn->lhp', pieces[3], carried, precision=highest)
        return (block_decay[:, None, None] * carried + own_state, inside + from_before)
    start_state = jnp.zeros((HEADS, HDIM, DSTATE), jnp.float32)
    _, outputs = lax.scan(advance, start_state, (inputs_f, steps_f, keys_f, queries_f))
    outputs = outputs + d_skip[None, None, :, None] * inputs_f
    gated_rows = (outputs.reshape(TOKENS, INNER) * jax.nn.silu(z_gate.astype(jnp.float32))).astype(jnp.bfloat16)
    group_rows = INNER // N_EXP
    mixed_sum = jnp.zeros((TOKENS, D), jnp.float32)
    for group_index in range(N_EXP):
        lower_row = group_index * group_rows
        partial_sum = jnp.dot(gated_rows[:, lower_row:lower_row + group_rows], out_proj[lower_row:lower_row + group_rows], preferred_element_type=jnp.float32)
        rounded = lax.optimization_barrier(partial_sum.astype(jnp.bfloat16))
        mixed_sum = mixed_sum + rounded.astype(jnp.float32)
    stream = mixed_sum + residual.astype(jnp.float32)
    mean_square = lax.optimization_barrier(jnp.mean(stream * stream, axis=1, keepdims=True))
    normed = (stream * lax.rsqrt(mean_square + epsilon) * norm_gain).astype(jnp.bfloat16)
    logits = jnp.dot(normed, router, preferred_element_type=jnp.float32).reshape(NBLK, BLOCK, EXPERTS)
    chosen = jnp.take_along_axis(logits, block_experts[:, None, :].astype(jnp.int32), axis=2)
    mixing_gates = jax.nn.sigmoid(chosen - chosen[:, :, ::-1])

    def one_block(pieces):
        rows_in, named_pair, gate_pair = pieces
        summed = jnp.zeros((BLOCK, D), jnp.float32)
        for which_slot in range(2):
            expert_index = named_pair[which_slot]
            gate_part = jnp.dot(rows_in, w_gate[expert_index], preferred_element_type=jnp.float32)
            up_part = jnp.dot(rows_in, w_up[expert_index], preferred_element_type=jnp.float32)
            hidden = (jax.nn.silu(gate_part) * up_part).astype(jnp.bfloat16)
            down_part = lax.dot_general(hidden, w_down[expert_index], (((1,), (1,)), ((), ())), preferred_element_type=jnp.float32)
            summed = summed + gate_pair[:, which_slot:which_slot + 1] * down_part
        return summed
    expert_rows = lax.map(one_block, (normed.reshape(NBLK, BLOCK, D), block_experts, mixing_gates))
    return (stream.astype(jnp.bfloat16), expert_rows.reshape(TOKENS, D).astype(jnp.bfloat16))
```

```python
import jax
import jax.numpy as jnp
from jax import lax
from jax.experimental import pallas as pl
from jax.experimental.pallas import tpu as pltpu
from jax.sharding import PartitionSpec as P


BLOCK = 128
CORES = 2
AHEAD = 4
LAG = 2

highest = lax.Precision.HIGHEST
epsilon = 1e-05
f32 = jnp.float32
bf16 = jnp.bfloat16


def block_terms(inputs_f, steps_f, keys_f, queries_f, head_rates):
    length = inputs_f.shape[0]
    log_decay = -head_rates[:, None] * steps_f
    running = jnp.cumsum(log_decay, axis=1)
    spread = running[:, :, None] - running[:, None, :]
    lower_part = jnp.arange(length)[:, None] >= jnp.arange(length)[None, :]
    weights = jnp.where(lower_part[None], jnp.exp(jnp.minimum(spread, 0.0)), 0.0)
    scores = jnp.dot(queries_f, keys_f.T, precision=highest)
    mixing = scores[None] * weights * steps_f[:, None, :]
    inside = jnp.einsum("hls,shp->lhp", mixing, inputs_f, precision=highest)
    carry_weight = jnp.exp(running[:, -1:] - running) * steps_f
    own_state = jnp.einsum("hs,shp,sn->hpn", carry_weight, inputs_f, keys_f, precision=highest)
    return (inside, own_state, jnp.exp(running), jnp.exp(running[:, -1]))


def swap_cores(a, ctx):
    return lax.ppermute(a, "ctx", [(i, i ^ 1) for i in range(ctx)])


def entering_state(own_state, decay, ctx, core, chip):
    chips = ctx // CORES
    heads, hdim, dstate = own_state.shape
    half = heads // CORES
    by_half = own_state.reshape(CORES, half * hdim, dstate)
    decay_half = decay.reshape(CORES, half)

    def pick(a, k):
        return lax.dynamic_index_in_dim(a, k, 0, False)

    def packed(state, rates):
        wide = jnp.broadcast_to(rates[:, None], (half, dstate))
        high = wide.astype(bf16)
        low = (wide - high.astype(f32)).astype(bf16)
        fill = (-2 * half) % 16
        rows = [state.astype(bf16), high, low]
        if fill:
            rows.append(jnp.zeros((fill, dstate), bf16))
        return jnp.concatenate(rows, 0)

    def opened(a):
        rows = half * hdim
        rates = a[rows : rows + half].astype(f32) + a[rows + half : rows + 2 * half].astype(f32)
        return a[:rows].astype(f32).reshape(half, hdim, dstate), rates[:, :1, None]

    mine = pick(by_half, core).reshape(half, hdim, dstate)
    mine_rate = pick(decay_half, core)[:, None, None]
    other, other_rate = opened(swap_cores(packed(pick(by_half, 1 - core), pick(decay_half, 1 - core)), ctx))
    first = core == 0
    first_state, first_rate = jnp.where(first, mine, other), jnp.where(first, mine_rate, other_rate)
    second_state, second_rate = jnp.where(first, other, mine), jnp.where(first, other_rate, mine_rate)
    total = second_rate * first_state + second_state
    message = packed(total.reshape(half * hdim, dstate), (first_rate * second_rate)[:, 0, 0])
    before = jnp.zeros_like(total)
    scale = jnp.ones((half, 1, 1), f32)
    for hop in range(1, chips):
        pairs = [
            (z * CORES + c, (z + hop) * CORES + c) for z in range(chips - hop) for c in range(CORES)
        ]
        state, rate = opened(lax.ppermute(message, "ctx", pairs))
        here = chip >= hop
        before = before + jnp.where(here, scale * state, 0.0)
        scale = jnp.where(here, scale * rate, scale)
    for_second = first_rate * before + first_state
    keep = jnp.where(first, before, for_second)
    give = jnp.where(first, for_second, before).astype(bf16)
    got = swap_cores(give.reshape(half * hdim, dstate), ctx).astype(f32).reshape(half, hdim, dstate)
    lower, upper = jnp.where(first, keep, got), jnp.where(first, got, keep)
    return jnp.concatenate([lower, upper], 0)


def gate_up_kernel(step, parts, table, *refs):
    xs, ws, outs = refs[:2], refs[2:10], refs[10:]
    for direction in range(2):
        exp = xs[direction].shape[0]
        rows = jnp.concatenate(
            [xs[direction][r ^ table[step, 8], 0] for r in range(exp)], 0
        )
        for owner in range(2):
            for kind in range(2):
                w = ws[direction * 4 + owner * 2 + kind][0]
                outs[owner][direction, kind] = jnp.dot(
                    rows, w, preferred_element_type=f32
                ).astype(bf16)


def gate_up(step, table, rows, w_gate, w_up, parts):
    exp, _, sub, width = rows.shape
    hidden = w_gate.shape[2] // parts
    x_spec = [
        pl.BlockSpec((exp, 1, sub, width), lambda g, t, d=d: (0, t[step, 4 + d], 0, 0))
        for d in range(2)
    ]
    w_spec = [
        pl.BlockSpec((1, width, hidden), lambda g, t, d=d, o=o: (t[step, d * 2 + o], 0, t[step, 6 + d]))
        for d in range(2)
        for o in range(2)
        for _ in range(2)
    ]
    shape = (2, 2, exp * sub, hidden)
    out = jax.ShapeDtypeStruct(shape, bf16)
    return pl.pallas_call(
        lambda *a: gate_up_kernel(step, parts, *a),
        out_shape=(out, out),
        grid_spec=pltpu.PrefetchScalarGridSpec(
            num_scalar_prefetch=1,
            grid=(1,),
            in_specs=x_spec + w_spec,
            out_specs=[pl.BlockSpec(shape, lambda g, t: (0, 0, 0, 0))] * 2,
        ),
        name=f"gate_up_{step}",
    )(table, rows, rows, *([w_gate, w_up] * 4))


def down_kernel(parts, table, own_ref, other_ref, w_own, w_other, out_ref):
    total = None
    width = own_ref.shape[2]
    for h_ref, w_ref in ((own_ref, w_own), (other_ref, w_other)):
        for q in range(parts):
            term = lax.dot_general(
                h_ref[q],
                w_ref[0, :, q * width : (q + 1) * width],
                (((1,), (1,)), ((), ())),
                preferred_element_type=f32,
            )
            total = term if total is None else total + term
    out_ref[0] = total.astype(bf16)


def down(table, own, other, w_down, blocks, parts):
    _, rows, width = own.shape
    h_spec = pl.BlockSpec((parts, rows, width), lambda b, t: (b, 0, 0))
    w_shape = (1,) + w_down.shape[1:]
    return pl.pallas_call(
        lambda *a: down_kernel(parts, *a),
        out_shape=jax.ShapeDtypeStruct((blocks, rows, w_down.shape[1]), bf16),
        grid_spec=pltpu.PrefetchScalarGridSpec(
            num_scalar_prefetch=1,
            grid=(blocks,),
            in_specs=[
                h_spec,
                h_spec,
                pl.BlockSpec(w_shape, lambda b, t: (t[0, b], 0, 0)),
                pl.BlockSpec(w_shape, lambda b, t: (t[1, b], 0, 0)),
            ],
            out_specs=pl.BlockSpec((1, rows, w_down.shape[1]), lambda b, t: (b, 0, 0)),
        ),
        name="down",
    )(table, own, other, w_down, w_down)


def per_device(
    x_in,
    z_gate,
    b_proj,
    c_proj,
    dt_raw,
    a_log,
    d_skip,
    out_proj,
    residual,
    norm_gain,
    router,
    w_gate,
    w_up,
    w_down,
    block_experts,
):
    ctx, exp = lax.axis_size("ctx"), lax.axis_size("exp")
    place, column = lax.axis_index("ctx"), lax.axis_index("exp")
    chip, core = place // CORES, place % CORES
    chips = ctx // CORES
    slab_rows = x_in.shape[0]
    head_count = dt_raw.shape[0]
    head_size = x_in.shape[1] // head_count
    blocks = block_experts.shape[0]
    half_blocks = blocks // 2
    model_width = residual.shape[1]
    width = model_width // ctx
    share = model_width // exp
    sub = slab_rows // exp
    expert_count = router.shape[1]
    parts = 2 if w_gate.shape[2] % 256 == 0 else 1
    hidden_cols = w_gate.shape[2] // parts
    chunks = half_blocks * parts
    steps = chunks + LAG * (chips - 1)

    step_ids = jnp.arange(steps)[:, None]
    starts = jnp.stack([LAG * (chips - 1 - chip), LAG * chip])[None, :]
    chunk_ids = jnp.clip(step_ids - starts, 0, chunks - 1)
    block_ids = chunk_ids // parts + jnp.arange(2)[None, :] * half_blocks
    named = block_experts[block_ids]
    of_core = jnp.stack([jnp.where(core == 0, named[:, :, 1], named[:, :, 0]),
                         jnp.where(core == 0, named[:, :, 0], named[:, :, 1])], -1)
    table = jnp.concatenate(
        [
            of_core.reshape(steps, 4),
            block_ids,
            chunk_ids % parts,
            jnp.broadcast_to(column, (steps, 1)),
        ],
        1,
    ).astype(jnp.int32)
    down_table = jnp.stack(
        [jnp.where(core == 0, block_experts[:, 0], block_experts[:, 1]),
         jnp.where(core == 0, block_experts[:, 1], block_experts[:, 0])]
    )

    head_rates = jnp.exp(a_log)
    steps_f = jax.nn.softplus(dt_raw)
    inputs_f = x_in.astype(f32).reshape(slab_rows, head_count, head_size)
    keys_f = b_proj.astype(f32)
    queries_f = c_proj.astype(f32)
    inside, own_state, entry_scale, block_decay = block_terms(
        inputs_f, steps_f, keys_f, queries_f, head_rates
    )
    entering = entering_state(own_state, block_decay, ctx, core, chip)
    from_before = entry_scale.T[..., None] * jnp.einsum(
        "ln,hpn->lhp", queries_f, entering, precision=highest
    )
    outputs = inside + from_before + d_skip[None, :, None] * inputs_f
    gated_rows = (outputs.reshape(slab_rows, -1) * jax.nn.silu(z_gate.astype(f32))).astype(bf16)
    group_term = jnp.dot(gated_rows, out_proj, preferred_element_type=f32).astype(bf16)

    def across(pieces, m):
        return lax.ppermute(
            lax.dynamic_index_in_dim(pieces, column ^ m, 0, False),
            "exp",
            [(j, j ^ m) for j in range(exp)],
        )

    by_rows = group_term.reshape(exp, sub, model_width)
    mixed = lax.dynamic_index_in_dim(by_rows, column, 0, False).astype(f32)
    for m in range(1, exp):
        mixed = mixed + across(by_rows, m).astype(f32)
    own_residual = lax.dynamic_slice_in_dim(residual, column * sub, sub, 0)
    stream = mixed + own_residual.astype(f32)
    mean_square = jnp.mean(stream * stream, axis=1, keepdims=True)
    normed = (stream * lax.rsqrt(mean_square + epsilon) * norm_gain).astype(bf16)
    logits = jnp.dot(normed, router, preferred_element_type=f32)
    named_here = lax.dynamic_index_in_dim(block_experts, place, 0, False)
    one_hot = (named_here[:, None] == jnp.arange(expert_count, dtype=jnp.int32)[None, :]).astype(f32)
    chosen = jnp.einsum("te,se->st", logits, one_hot, precision=highest)
    gates = jax.nn.sigmoid(chosen - chosen[::-1])
    gates_high = gates.astype(bf16)
    gates_low = (gates - gates_high.astype(f32)).astype(bf16)
    gate_rows = jnp.concatenate([gates_high, gates_low], 0)

    stream_rows = stream.astype(bf16).reshape(sub, exp, share).transpose(1, 0, 2)
    stream_out = jnp.zeros((exp, sub, share), bf16)
    stream_out = lax.dynamic_update_index_in_dim(
        stream_out, lax.dynamic_index_in_dim(stream_rows, column, 0, False), column, 0
    )
    for m in range(1, exp):
        stream_out = lax.dynamic_update_index_in_dim(
            stream_out, across(stream_rows, m), column ^ m, 0
        )
    stream_out = stream_out.reshape(slab_rows, share)

    extra = jnp.pad(gate_rows, ((0, 12), (0, width - sub)))
    pieces = jnp.concatenate(
        [
            normed.reshape(sub, ctx, width).transpose(1, 0, 2),
            jnp.broadcast_to(extra[None], (ctx, 16, width)),
        ],
        1,
    )
    slabs = lax.all_to_all(pieces, "ctx", split_axis=0, concat_axis=0, tiled=True)
    normed_part = slabs[:, :sub]
    gate_part = slabs[:, sub : sub + 4, :sub].astype(f32)
    gate_part = (gate_part[:, :2] + gate_part[:, 2:]).astype(bf16)
    flat = jnp.concatenate(
        [
            normed_part.reshape(ctx * sub, width),
            jnp.pad(gate_part.reshape(ctx * 2, sub), ((0, (-2 * ctx) % 16), (0, width - sub))),
        ],
        0,
    )
    received = [flat] + [
        lax.ppermute(flat, "exp", [(j, j ^ m) for j in range(exp)]) for m in range(1, exp)
    ]
    everyone = jnp.concatenate(received, 0).reshape(exp, -1, width)
    rows = everyone[:, : ctx * sub].reshape(exp, ctx, sub, width)
    all_gates = everyone[:, ctx * sub : ctx * sub + 2 * ctx, :sub].reshape(exp, ctx, 2, sub)
    all_gates = jnp.take(all_gates, column ^ jnp.arange(exp), axis=0)
    all_gates = lax.dynamic_index_in_dim(all_gates, core, 2, False)
    all_gates = all_gates.transpose(1, 0, 2).reshape(ctx, slab_rows, 1).astype(f32)
    at_bottom = chip == 0
    end_gates = lax.dynamic_slice_in_dim(
        all_gates, jnp.where(at_bottom, 0, half_blocks), half_blocks, 0
    )

    def pairs_of(step, delta, lag, count):
        pairs = []
        for z in range(chips):
            start = lag * (chips - 1 - z if delta < 0 else z)
            if 0 <= z + delta < chips and 0 <= step - start < count:
                pairs += [(z * CORES + c, (z + delta) * CORES + c) for c in range(CORES)]
        return pairs

    def hop(a, step, delta, lag=LAG, count=chunks):
        pairs = pairs_of(step, delta, lag, count)
        return lax.ppermute(a, "ctx", pairs) if pairs else jnp.zeros_like(a)

    arrived = {}
    finals = []
    for step in range(steps):
        if step >= AHEAD:
            table, _ = lax.optimization_barrier((table, arrived[step - AHEAD, 0]))
        theirs, mine = gate_up(step, table, rows, w_gate, w_up, parts)
        other = swap_cores(theirs, ctx)
        carried = []
        for d, delta in enumerate((-1, 1)):
            total = mine[d].astype(f32) + other[d].astype(f32)
            if step >= LAG:
                total = total + arrived[step - LAG, d].astype(f32)
            carried.append(total)
            arrived[step, d] = hop(total.astype(bf16), step, delta)
        if step >= LAG * (chips - 1):
            n = step - LAG * (chips - 1)
            done = jnp.where(at_bottom, carried[0], carried[1])
            hidden = (jax.nn.silu(done[0]) * done[1] * end_gates[n // parts]).astype(bf16)
            finals.append(hidden)

    slots = 2 * chunks
    store = jnp.zeros((slots + parts, slab_rows, hidden_cols), bf16)
    came = {}
    at_top = chip == chips - 1
    for step in range(chunks + (chips - 2)):
        for d, (delta, at_start, first) in enumerate(((1, at_bottom, chip), (-1, at_top, chips - 1 - chip))):
            send = finals[min(step, chunks - 1)]
            if step >= 1:
                send = jnp.where(at_start, send, came[step - 1, d])
            got = hop(send, step, delta, 1)
            came[step, d] = got
            index = step - (first - 1)
            kept = got
            if step < chunks:
                kept = jnp.where(at_start, finals[step], got)
                index = jnp.where(at_start, step, index)
            else:
                index = jnp.where(at_start, chunks, index)
            index = jnp.where((index < 0) | (index >= chunks), slots, index + d * chunks)
            store = lax.dynamic_update_index_in_dim(store, kept, index, 0)
    other_store = swap_cores(store, ctx)
    out_part = down(down_table, store, other_store, w_down, blocks, parts)

    per = blocks // exp
    grouped = out_part.reshape(exp, per, slab_rows, width)
    owned = lax.dynamic_index_in_dim(grouped, column, 0, False).astype(f32)
    for m in range(1, exp):
        owned = owned + across(grouped, m).astype(f32)
    owned = owned.astype(bf16)
    result = jnp.zeros((per, slab_rows, width), bf16)
    for r in range(per):
        pairs = []
        for i in range(ctx):
            for j in range(exp):
                pairs.append((i * exp + j, (j * per + ((i % per) ^ r)) * exp + i // per))
        piece = lax.dynamic_index_in_dim(owned, (place % per) ^ r, 0, False)
        got = lax.ppermute(piece, ("ctx", "exp"), pairs)
        result = lax.dynamic_update_index_in_dim(result, got, (place % per) ^ r, 0)
    expert_out = result.transpose(1, 0, 2).reshape(slab_rows, share)
    return (stream_out, expert_out)


def solution(mesh):
    placed = (
        P("ctx", "exp"),
        P("ctx", "exp"),
        P("ctx", None),
        P("ctx", None),
        P("exp", "ctx"),
        P("exp"),
        P("exp"),
        P("exp", None),
        P("ctx", None),
        P(),
        P(),
        P(None, "ctx", "exp"),
        P(None, "ctx", "exp"),
        P(None, "ctx", "exp"),
        P(),
    )
    return jax.shard_map(
        per_device,
        mesh=mesh,
        in_specs=placed,
        out_specs=(P("ctx", "exp"), P("ctx", "exp")),
        check_vma=False,
    )
```

```python
import jax
import jax.numpy as jnp
from jax import lax
from jax.experimental import pallas as pl
from jax.experimental.pallas import tpu as pltpu
from jax.sharding import PartitionSpec as P


BLOCK = 128
CORES = 2
LAG = 2

highest = lax.Precision.HIGHEST
epsilon = 1e-05
f32 = jnp.float32
bf16 = jnp.bfloat16


def block_terms(inputs_f, steps_f, keys_f, queries_f, head_rates):
    length = inputs_f.shape[0]
    log_decay = -head_rates[:, None] * steps_f
    running = jnp.cumsum(log_decay, axis=1)
    spread = running[:, :, None] - running[:, None, :]
    lower_part = jnp.arange(length)[:, None] >= jnp.arange(length)[None, :]
    weights = jnp.where(lower_part[None], jnp.exp(jnp.minimum(spread, 0.0)), 0.0)
    scores = jnp.dot(queries_f, keys_f.T, precision=highest)
    mixing = scores[None] * weights * steps_f[:, None, :]
    inside = jnp.einsum("hls,shp->lhp", mixing, inputs_f, precision=highest)
    carry_weight = jnp.exp(running[:, -1:] - running) * steps_f
    own_state = jnp.einsum("hs,shp,sn->hpn", carry_weight, inputs_f, keys_f, precision=highest)
    return (inside, own_state, jnp.exp(running), jnp.exp(running[:, -1]))


def swap_cores(a, ctx):
    return lax.ppermute(a, "ctx", [(i, i ^ 1) for i in range(ctx)])


def entering_state(own_state, decay, ctx, core, chip):
    chips = ctx // CORES
    heads, hdim, dstate = own_state.shape
    half = heads // CORES
    by_half = own_state.reshape(CORES, half * hdim, dstate)
    decay_half = decay.reshape(CORES, half)

    def pick(a, k):
        return lax.dynamic_index_in_dim(a, k, 0, False)

    def packed(state, rates):
        wide = jnp.broadcast_to(rates[:, None], (half, dstate))
        high = wide.astype(bf16)
        low = (wide - high.astype(f32)).astype(bf16)
        fill = (-2 * half) % 16
        rows = [state.astype(bf16), high, low]
        if fill:
            rows.append(jnp.zeros((fill, dstate), bf16))
        return jnp.concatenate(rows, 0)

    def opened(a):
        rows = half * hdim
        rates = a[rows : rows + half].astype(f32) + a[rows + half : rows + 2 * half].astype(f32)
        return a[:rows].astype(f32).reshape(half, hdim, dstate), rates[:, :1, None]

    mine = pick(by_half, core).reshape(half, hdim, dstate)
    mine_rate = pick(decay_half, core)[:, None, None]
    other, other_rate = opened(swap_cores(packed(pick(by_half, 1 - core), pick(decay_half, 1 - core)), ctx))
    first = core == 0
    first_state, first_rate = jnp.where(first, mine, other), jnp.where(first, mine_rate, other_rate)
    second_state, second_rate = jnp.where(first, other, mine), jnp.where(first, other_rate, mine_rate)
    total = second_rate * first_state + second_state
    message = packed(total.reshape(half * hdim, dstate), (first_rate * second_rate)[:, 0, 0])
    before = jnp.zeros_like(total)
    scale = jnp.ones((half, 1, 1), f32)
    for hop in range(1, chips):
        pairs = [
            (z * CORES + c, (z + hop) * CORES + c) for z in range(chips - hop) for c in range(CORES)
        ]
        state, rate = opened(lax.ppermute(message, "ctx", pairs))
        here = chip >= hop
        before = before + jnp.where(here, scale * state, 0.0)
        scale = jnp.where(here, scale * rate, scale)
    for_second = first_rate * before + first_state
    keep = jnp.where(first, before, for_second)
    give = jnp.where(first, for_second, before).astype(bf16)
    got = swap_cores(give.reshape(half * hdim, dstate), ctx).astype(f32).reshape(half, hdim, dstate)
    lower, upper = jnp.where(first, keep, got), jnp.where(first, got, keep)
    return jnp.concatenate([lower, upper], 0)


def step_kernel(step, info, table, *refs):
    first, last, has_arrived, ends = info
    refs = list(refs)
    x_ref, wg_ref, wu_ref = refs[:3]
    del refs[:3]
    other_ref = None if first else refs.pop(0)
    arrived = [refs.pop(0), refs.pop(0)] if has_arrived else None
    gate_ref = refs.pop(0) if ends else None
    ahead_ref = None if last else refs.pop(0)
    carry = None if first else [refs.pop(0), refs.pop(0)]
    hidden_ref = refs.pop(0) if ends else None
    exp = x_ref.shape[0]
    product = pl.program_id(0) + (2 if last else 0)

    def products():
        rows = jnp.concatenate([x_ref[r ^ table[step, 16], 0] for r in range(exp)], 0)
        return [jnp.dot(rows, w[0], preferred_element_type=f32) for w in (wg_ref, wu_ref)]

    if not last:

        @pl.when((product < 2) & (table[step, 12 + jnp.minimum(product, 1)] == 1))
        def _():
            slot = jnp.minimum(product, 1)
            for kind, value in enumerate(products()):
                ahead_ref[slot, kind] = value.astype(bf16)

    if not first:
        for d in range(2):

            @pl.when((product == 2 + d) & (table[step, 14 + d] == 1))
            def _():
                totals = []
                for kind, value in enumerate(products()):
                    value = value + other_ref[d, kind].astype(f32)
                    if has_arrived:
                        value = value + arrived[d][kind].astype(f32)
                    carry[d][kind] = value.astype(bf16)
                    totals.append(value)
                if ends:

                    @pl.when(table[step, 17 + d] == 1)
                    def _():
                        gate, up = totals
                        hidden_ref[...] = (jax.nn.silu(gate) * up * gate_ref[0]).astype(bf16)


def step_products(step, steps, chips, table, rows, w_gate, w_up, parts, other, arrived, end_gates):
    exp, _, sub, width = rows.shape
    hidden = w_gate.shape[2] // parts
    first, last = step < 0, step == steps - 1
    ends = step >= LAG * (chips - 1)
    base = 2 if last else 0
    row = step + 1
    count = 2 if (first or last) else 4

    x_spec = pl.BlockSpec((exp, 1, sub, width), lambda g, t: (0, t[row, 4 + g + base], 0, 0))
    w_spec = pl.BlockSpec((1, width, hidden), lambda g, t: (t[row, g + base], 0, t[row, 8 + g + base]))
    shape = (2, exp * sub, hidden)
    whole = lambda shape: pl.BlockSpec(shape, lambda g, t: (0,) * len(shape))
    in_specs, args = [x_spec, w_spec, w_spec], [rows, w_gate, w_up]
    if not first:
        in_specs.append(whole((2,) + shape))
        args.append(other)
    if arrived is not None:
        in_specs += [whole(shape)] * 2
        args += list(arrived)
    if ends:
        unit = (step - LAG * (chips - 1)) // parts
        in_specs.append(pl.BlockSpec((1,) + end_gates.shape[1:], lambda g, t: (unit, 0, 0)))
        args.append(end_gates)
    out_specs, out_shape = [], []
    if not last:
        out_specs.append(whole((2,) + shape))
        out_shape.append(jax.ShapeDtypeStruct((2,) + shape, bf16))
    if not first:
        out_specs += [whole(shape)] * 2
        out_shape += [jax.ShapeDtypeStruct(shape, bf16)] * 2
    if ends:
        out_specs.append(whole(shape[1:]))
        out_shape.append(jax.ShapeDtypeStruct(shape[1:], bf16))
    info = (first, last, arrived is not None, ends)
    out = pl.pallas_call(
        lambda *a: step_kernel(row, info, *a),
        out_shape=out_shape,
        grid_spec=pltpu.PrefetchScalarGridSpec(
            num_scalar_prefetch=1, grid=(count,), in_specs=in_specs, out_specs=out_specs
        ),
        name=f"products_{row}",
    )(table, *args)
    out = list(out)
    ahead = None if last else out.pop(0)
    carry = None if first else (out.pop(0), out.pop(0))
    return ahead, carry, (out.pop(0) if ends else None)


def down_kernel(near_blocks, parts, table, *refs):
    near, near_other, far, far_other, w_own, w_other, out_ref = refs
    g = pl.program_id(0)
    block = g % near_blocks
    width = near.shape[2]
    for side, pair in enumerate(((near, near_other), (far, far_other))):

        @pl.when(g // near_blocks == side)
        def _():
            total = None
            for h_ref, w_ref in zip(pair, (w_own, w_other)):
                for q in range(parts):
                    term = lax.dot_general(
                        h_ref[block * parts + q],
                        w_ref[0, :, q * width : (q + 1) * width],
                        (((1,), (1,)), ((), ())),
                        preferred_element_type=f32,
                    )
                    total = term if total is None else total + term
            out_ref[0, 0] = total.astype(bf16)


def down(pair, table, near, far, near_other, far_other, w_down, parts):
    count, rows, width = near.shape
    near_blocks = count // parts
    base = pair * 2 * near_blocks
    whole = pl.BlockSpec(near.shape, lambda g, t: (0, 0, 0))
    w_shape = (1,) + w_down.shape[1:]
    return pl.pallas_call(
        lambda *a: down_kernel(near_blocks, parts, *a),
        out_shape=jax.ShapeDtypeStruct((2, near_blocks, rows, w_down.shape[1]), bf16),
        grid_spec=pltpu.PrefetchScalarGridSpec(
            num_scalar_prefetch=1,
            grid=(2 * near_blocks,),
            in_specs=[
                whole,
                whole,
                whole,
                whole,
                pl.BlockSpec(w_shape, lambda g, t: (t[0, base + g], 0, 0)),
                pl.BlockSpec(w_shape, lambda g, t: (t[1, base + g], 0, 0)),
            ],
            out_specs=pl.BlockSpec(
                (1, 1, rows, w_down.shape[1]),
                lambda g, t: (t[2, base + g], g % near_blocks, 0, 0),
            ),
        ),
        name=f"down_{pair}",
    )(table, near, near_other, far, far_other, w_down, w_down)


def per_device(
    x_in,
    z_gate,
    b_proj,
    c_proj,
    dt_raw,
    a_log,
    d_skip,
    out_proj,
    residual,
    norm_gain,
    router,
    w_gate,
    w_up,
    w_down,
    block_experts,
):
    ctx, exp = lax.axis_size("ctx"), lax.axis_size("exp")
    place, column = lax.axis_index("ctx"), lax.axis_index("exp")
    chip, core = place // CORES, place % CORES
    chips = ctx // CORES
    slab_rows = x_in.shape[0]
    head_count = dt_raw.shape[0]
    head_size = x_in.shape[1] // head_count
    blocks = block_experts.shape[0]
    half_blocks = blocks // 2
    model_width = residual.shape[1]
    width = model_width // ctx
    share = model_width // exp
    sub = slab_rows // exp
    expert_count = router.shape[1]
    parts = 2 if w_gate.shape[2] % 256 == 0 else 1
    chunks = half_blocks * parts
    steps = chunks + LAG * (chips - 1)

    step_ids = jnp.arange(steps + 1)[:, None]
    starts = jnp.stack([LAG * (chips - 1 - chip), LAG * chip])[None, :]
    raw_ids = step_ids - starts
    wanted = ((raw_ids >= 0) & (raw_ids < chunks)).astype(jnp.int32)
    chunk_ids = jnp.clip(raw_ids, 0, chunks - 1)
    block_ids = chunk_ids // parts + jnp.arange(2)[None, :] * half_blocks
    part_ids = chunk_ids % parts
    named = block_experts[block_ids]
    of_mine = jnp.where(core == 0, named[:, :, 0], named[:, :, 1])
    of_other = jnp.where(core == 0, named[:, :, 1], named[:, :, 0])

    def joined(ahead, own):
        return jnp.concatenate([ahead, jnp.roll(own, 1, axis=0)], 1)

    place_columns = jnp.stack(
        [column, (chip == 0).astype(jnp.int32), (chip == chips - 1).astype(jnp.int32)]
    )
    table = jnp.concatenate(
        [
            joined(of_other, of_mine),
            joined(block_ids, block_ids),
            joined(part_ids, part_ids),
            joined(wanted, wanted),
            jnp.broadcast_to(place_columns[None], (steps + 1, 3)),
        ],
        1,
    ).astype(jnp.int32)
    near_half = jnp.where(chip < chips // 2, 0, 1)
    near_blocks = 2 // parts
    pairs_count = chunks // 2
    halves = jnp.stack([near_half, 1 - near_half])
    down_blocks = (
        halves[None, :, None] * half_blocks
        + (jnp.arange(pairs_count)[:, None] * near_blocks + jnp.arange(near_blocks)[None])[:, None]
    ).reshape(-1)
    named_down = block_experts[down_blocks]
    down_table = jnp.stack(
        [
            jnp.where(core == 0, named_down[:, 0], named_down[:, 1]),
            jnp.where(core == 0, named_down[:, 1], named_down[:, 0]),
            jnp.broadcast_to(halves[None, :, None], (pairs_count, 2, near_blocks)).reshape(-1),
        ]
    ).astype(jnp.int32)

    head_rates = jnp.exp(a_log)
    steps_f = jax.nn.softplus(dt_raw)
    inputs_f = x_in.astype(f32).reshape(slab_rows, head_count, head_size)
    keys_f = b_proj.astype(f32)
    queries_f = c_proj.astype(f32)
    inside, own_state, entry_scale, block_decay = block_terms(
        inputs_f, steps_f, keys_f, queries_f, head_rates
    )
    entering = entering_state(own_state, block_decay, ctx, core, chip)
    from_before = entry_scale.T[..., None] * jnp.einsum(
        "ln,hpn->lhp", queries_f, entering, precision=highest
    )
    outputs = inside + from_before + d_skip[None, :, None] * inputs_f
    gated_rows = (outputs.reshape(slab_rows, -1) * jax.nn.silu(z_gate.astype(f32))).astype(bf16)
    group_term = jnp.dot(gated_rows, out_proj, preferred_element_type=f32).astype(bf16)

    def across(pieces, m):
        return lax.ppermute(
            lax.dynamic_index_in_dim(pieces, column ^ m, 0, False),
            "exp",
            [(j, j ^ m) for j in range(exp)],
        )

    by_rows = group_term.reshape(exp, sub, model_width)
    mixed = lax.dynamic_index_in_dim(by_rows, column, 0, False).astype(f32)
    for m in range(1, exp):
        mixed = mixed + across(by_rows, m).astype(f32)
    own_residual = lax.dynamic_slice_in_dim(residual, column * sub, sub, 0)
    stream = mixed + own_residual.astype(f32)
    mean_square = jnp.mean(stream * stream, axis=1, keepdims=True)
    normed = (stream * lax.rsqrt(mean_square + epsilon) * norm_gain).astype(bf16)
    logits = jnp.dot(normed, router, preferred_element_type=f32)
    named_here = lax.dynamic_index_in_dim(block_experts, place, 0, False)
    one_hot = (named_here[:, None] == jnp.arange(expert_count, dtype=jnp.int32)[None, :]).astype(f32)
    chosen = jnp.einsum("te,se->st", logits, one_hot, precision=highest)
    gates = jax.nn.sigmoid(chosen - chosen[::-1])
    gates_high = gates.astype(bf16)
    gates_low = (gates - gates_high.astype(f32)).astype(bf16)
    gate_rows = jnp.concatenate([gates_high, gates_low], 0)

    stream_rows = stream.astype(bf16).reshape(sub, exp, share).transpose(1, 0, 2)
    stream_out = jnp.zeros((exp, sub, share), bf16)
    stream_out = lax.dynamic_update_index_in_dim(
        stream_out, lax.dynamic_index_in_dim(stream_rows, column, 0, False), column, 0
    )
    for m in range(1, exp):
        stream_out = lax.dynamic_update_index_in_dim(
            stream_out, across(stream_rows, m), column ^ m, 0
        )
    stream_out = stream_out.reshape(slab_rows, share)

    extra = jnp.pad(gate_rows, ((0, 12), (0, width - sub)))
    pieces = jnp.concatenate(
        [
            normed.reshape(sub, ctx, width).transpose(1, 0, 2),
            jnp.broadcast_to(extra[None], (ctx, 16, width)),
        ],
        1,
    )
    slabs = lax.all_to_all(pieces, "ctx", split_axis=0, concat_axis=0, tiled=True)
    normed_part = slabs[:, :sub]
    gate_part = slabs[:, sub : sub + 4, :sub].astype(f32)
    gate_part = (gate_part[:, :2] + gate_part[:, 2:]).astype(bf16)
    flat = jnp.concatenate(
        [
            normed_part.reshape(ctx * sub, width),
            jnp.pad(gate_part.reshape(ctx * 2, sub), ((0, (-2 * ctx) % 16), (0, width - sub))),
        ],
        0,
    )
    received = [flat] + [
        lax.ppermute(flat, "exp", [(j, j ^ m) for j in range(exp)]) for m in range(1, exp)
    ]
    everyone = jnp.concatenate(received, 0).reshape(exp, -1, width)
    rows = everyone[:, : ctx * sub].reshape(exp, ctx, sub, width)
    all_gates = everyone[:, ctx * sub : ctx * sub + 2 * ctx, :sub].reshape(exp, ctx, 2, sub)
    all_gates = jnp.take(all_gates, column ^ jnp.arange(exp), axis=0)
    all_gates = lax.dynamic_index_in_dim(all_gates, core, 2, False)
    all_gates = all_gates.transpose(1, 0, 2).reshape(ctx, slab_rows, 1).astype(f32)
    at_bottom = chip == 0
    end_gates = lax.dynamic_slice_in_dim(
        all_gates, jnp.where(at_bottom, 0, half_blocks), half_blocks, 0
    )

    def hop(a, step, delta):
        pairs = []
        for z in range(chips):
            start = LAG * (chips - 1 - z if delta < 0 else z)
            if 0 <= z + delta < chips and 0 <= step - start < chunks:
                pairs += [(z * CORES + c, (z + delta) * CORES + c) for c in range(CORES)]
        return lax.ppermute(a, "ctx", pairs) if pairs else None

    def spread(a, u):
        pairs = []
        for c in range(CORES):
            pairs.append((u * CORES + c, (u + 1) * CORES + c))
            pairs.append(((chips - 1 - u) * CORES + c, (chips - 2 - u) * CORES + c))
        return lax.ppermute(a, "ctx", pairs)

    ahead, _, _ = step_products(-1, steps, chips, table, rows, w_gate, w_up, parts, None, None, None)
    arrived = {}
    finals = []
    outs = []
    nearness = jnp.minimum(chip, chips - 1 - chip)
    for step in range(steps):
        other = swap_cores(ahead, ctx)
        came = None
        if step >= LAG and arrived[step - LAG][0] is not None:
            came = arrived[step - LAG]
        ahead, carry, hidden = step_products(
            step, steps, chips, table, rows, w_gate, w_up, parts, other, came, end_gates
        )
        arrived[step] = (hop(carry[0], step, -1), hop(carry[1], step, 1))
        if hidden is not None:
            finals.append(hidden)
            if len(finals) % 2 == 0:
                reach = [jnp.stack(finals[-2:])]
                for u in range(chips - 1):
                    reach.append(spread(reach[-1], u))
                near, far = reach[0], reach[chips - 1]
                for u in range(1, chips // 2):
                    near = jnp.where(nearness == u, reach[u], near)
                    far = jnp.where(nearness == u, reach[chips - 1 - u], far)
                outs.append(
                    down(
                        len(outs), down_table, near, far,
                        swap_cores(near, ctx), swap_cores(far, ctx), w_down, parts,
                    )
                )
    out_part = jnp.stack(outs, 1).reshape(blocks, slab_rows, width)

    per = blocks // exp
    grouped = out_part.reshape(exp, per, slab_rows, width)
    owned = lax.dynamic_index_in_dim(grouped, column, 0, False).astype(f32)
    for m in range(1, exp):
        owned = owned + across(grouped, m).astype(f32)
    owned = owned.astype(bf16)
    result = jnp.zeros((per, slab_rows, width), bf16)
    for r in range(per):
        pairs = []
        for i in range(ctx):
            for j in range(exp):
                pairs.append((i * exp + j, (j * per + ((i % per) ^ r)) * exp + i // per))
        piece = lax.dynamic_index_in_dim(owned, (place % per) ^ r, 0, False)
        got = lax.ppermute(piece, ("ctx", "exp"), pairs)
        result = lax.dynamic_update_index_in_dim(result, got, (place % per) ^ r, 0)
    expert_out = result.transpose(1, 0, 2).reshape(slab_rows, share)
    return (stream_out, expert_out)


def solution(mesh):
    placed = (
        P("ctx", "exp"),
        P("ctx", "exp"),
        P("ctx", None),
        P("ctx", None),
        P("exp", "ctx"),
        P("exp"),
        P("exp"),
        P("exp", None),
        P("ctx", None),
        P(),
        P(),
        P(None, "ctx", "exp"),
        P(None, "ctx", "exp"),
        P(None, "ctx", "exp"),
        P(),
    )
    return jax.shard_map(
        per_device,
        mesh=mesh,
        in_specs=placed,
        out_specs=(P("ctx", "exp"), P("ctx", "exp")),
        check_vma=False,
    )
```

```python
import jax
import jax.numpy as jnp
from jax import lax
from jax.experimental import pallas as pl
from jax.experimental.pallas import tpu as pltpu
from jax.sharding import PartitionSpec as P


CORES = 2
LAG = 2

highest = lax.Precision.HIGHEST
epsilon = 1e-05
f32 = jnp.float32
bf16 = jnp.bfloat16


def block_terms(inputs_f, steps_f, keys_f, queries_f, head_rates):
    length = inputs_f.shape[0]
    log_decay = -head_rates[:, None] * steps_f
    running = jnp.cumsum(log_decay, axis=1)
    spread = running[:, :, None] - running[:, None, :]
    lower_part = jnp.arange(length)[:, None] >= jnp.arange(length)[None, :]
    weights = jnp.where(lower_part[None], jnp.exp(jnp.minimum(spread, 0.0)), 0.0)
    scores = jnp.dot(queries_f, keys_f.T, precision=highest)
    mixing = scores[None] * weights * steps_f[:, None, :]
    inside = jnp.einsum("hls,shp->lhp", mixing, inputs_f, precision=highest)
    carry_weight = jnp.exp(running[:, -1:] - running) * steps_f
    own_state = jnp.einsum("hs,shp,sn->hpn", carry_weight, inputs_f, keys_f, precision=highest)
    return (inside, own_state, jnp.exp(running), jnp.exp(running[:, -1]))


def groups_of(chunks):
    groups = {}
    size = max(2, chunks // 8 * 2)
    for done in range(size, chunks - 2, size):
        groups[done] = (len(groups), size)
    groups[chunks - 2] = (len(groups), chunks - 2 - size * len(groups))
    groups[chunks - 1] = (len(groups), 1)
    groups[chunks] = (len(groups), 1)
    return groups


def swap_cores(a, ctx):
    return lax.ppermute(a, "ctx", [(i, i ^ 1) for i in range(ctx)])


def entering_state(own_state, decay, ctx, core, chip):
    chips = ctx // CORES
    heads, hdim, dstate = own_state.shape
    half = heads // CORES
    by_half = own_state.reshape(CORES, half * hdim, dstate)
    decay_half = decay.reshape(CORES, half)

    def pick(a, k):
        return lax.dynamic_index_in_dim(a, k, 0, False)

    def packed(state, rates):
        wide = jnp.broadcast_to(rates[:, None], (half, dstate))
        high = wide.astype(bf16)
        low = (wide - high.astype(f32)).astype(bf16)
        fill = (-2 * half) % 16
        rows = [state.astype(bf16), high, low]
        if fill:
            rows.append(jnp.zeros((fill, dstate), bf16))
        return jnp.concatenate(rows, 0)

    def opened(a):
        rows = half * hdim
        rates = a[rows : rows + half].astype(f32) + a[rows + half : rows + 2 * half].astype(f32)
        return a[:rows].astype(f32).reshape(half, hdim, dstate), rates[:, :1, None]

    mine = pick(by_half, core).reshape(half, hdim, dstate)
    mine_rate = pick(decay_half, core)[:, None, None]
    other, other_rate = opened(swap_cores(packed(pick(by_half, 1 - core), pick(decay_half, 1 - core)), ctx))
    first = core == 0
    first_state, first_rate = jnp.where(first, mine, other), jnp.where(first, mine_rate, other_rate)
    second_state, second_rate = jnp.where(first, other, mine), jnp.where(first, other_rate, mine_rate)
    total = second_rate * first_state + second_state
    message = packed(total.reshape(half * hdim, dstate), (first_rate * second_rate)[:, 0, 0])
    before = jnp.zeros_like(total)
    scale = jnp.ones((half, 1, 1), f32)
    for hop in range(1, chips):
        pairs = [
            (z * CORES + c, (z + hop) * CORES + c) for z in range(chips - hop) for c in range(CORES)
        ]
        state, rate = opened(lax.ppermute(message, "ctx", pairs))
        here = chip >= hop
        before = before + jnp.where(here, scale * state, 0.0)
        scale = jnp.where(here, scale * rate, scale)
    for_second = first_rate * before + first_state
    keep = jnp.where(first, before, for_second)
    give = jnp.where(first, for_second, before).astype(bf16)
    got = swap_cores(give.reshape(half * hdim, dstate), ctx).astype(f32).reshape(half, hdim, dstate)
    lower, upper = jnp.where(first, keep, got), jnp.where(first, got, keep)
    return jnp.concatenate([lower, upper], 0)


def step_kernel(row, parts, info, table, *refs):
    first, last, has_arrived, ends = info
    refs = list(refs)
    x_ref, wg_ref, wu_ref = refs[:3]
    del refs[:3]
    other_ref = None if first else refs.pop(0)
    arrived_ref = refs.pop(0) if has_arrived else None
    gate_ref = refs.pop(0) if ends else None
    ahead_ref = None if last else refs.pop(0)
    carry_ref = None if first else refs.pop(0)
    hidden_ref = refs.pop(0) if ends else None
    exp = x_ref.shape[0]
    is_own = pl.program_id(0) >= (0 if last else parts)

    def products():
        rows = jnp.concatenate([x_ref[r ^ table[row, 6], 0] for r in range(exp)], 0)
        return [jnp.dot(rows, w[0], preferred_element_type=f32) for w in (wg_ref, wu_ref)]

    if not last:

        @pl.when(jnp.logical_not(is_own) & (table[row, 4] == 1))
        def _():
            for kind, value in enumerate(products()):
                ahead_ref[kind] = value.astype(bf16)

    if not first:

        @pl.when(is_own & (table[row, 5] == 1))
        def _():
            totals = []
            for kind, value in enumerate(products()):
                value = value + other_ref[kind].astype(f32)
                if has_arrived:
                    value = value + arrived_ref[kind].astype(f32)
                carry_ref[kind] = value.astype(bf16)
                totals.append(value)
            if ends:

                @pl.when(table[row, 7] == 1)
                def _():
                    gate, up = totals
                    hidden_ref[...] = (jax.nn.silu(gate) * up * gate_ref[0]).astype(bf16)


def step_products(step, steps, chips, table, rows, w_gate, w_up, other, arrived, end_gates):
    exp, _, sub, width = rows.shape
    hidden = w_gate.shape[2]
    parts = 2 if hidden % 256 == 0 else 1
    cols = hidden // parts
    first, last = step < 0, step == steps - 1
    ends = step >= LAG * (chips - 1)
    row = step + 1
    phase0 = 1 if last else 0
    grid = parts if (first or last) else 2 * parts

    def which(g):
        return g // parts + phase0

    x_spec = pl.BlockSpec((exp, 1, sub, width), lambda g, t: (0, t[row, 2 + which(g)], 0, 0))
    w_spec = pl.BlockSpec((1, width, cols), lambda g, t: (t[row, which(g)], 0, g % parts))
    block = (2, exp * sub, cols)
    shape = (2, exp * sub, hidden)

    def own_part(g):
        return g if last else jnp.maximum(g - parts, 0)

    ahead_spec = pl.BlockSpec(block, lambda g, t: (0, 0, jnp.minimum(g, parts - 1)))
    own_spec = pl.BlockSpec(block, lambda g, t: (0, 0, own_part(g)))
    in_specs, args = [x_spec, w_spec, w_spec], [rows, w_gate, w_up]
    if not first:
        in_specs.append(own_spec)
        args.append(other)
    if arrived is not None:
        in_specs.append(own_spec)
        args.append(arrived)
    if ends:
        chunk = step - LAG * (chips - 1)
        in_specs.append(pl.BlockSpec((1,) + end_gates.shape[1:], lambda g, t: (chunk, 0, 0)))
        args.append(end_gates)
    out_specs, out_shape = [], []
    if not last:
        out_specs.append(ahead_spec)
        out_shape.append(jax.ShapeDtypeStruct(shape, bf16))
    if not first:
        out_specs.append(own_spec)
        out_shape.append(jax.ShapeDtypeStruct(shape, bf16))
    if ends:
        out_specs.append(pl.BlockSpec(block[1:], lambda g, t: (0, own_part(g))))
        out_shape.append(jax.ShapeDtypeStruct(shape[1:], bf16))
    info = (first, last, arrived is not None, ends)
    out = pl.pallas_call(
        lambda *a: step_kernel(row, parts, info, *a),
        out_shape=out_shape,
        grid_spec=pltpu.PrefetchScalarGridSpec(
            num_scalar_prefetch=1, grid=(grid,), in_specs=in_specs, out_specs=out_specs
        ),
    )(table, *args)
    out = list(out)
    ahead = None if last else out.pop(0)
    carry = None if first else out.pop(0)
    return ahead, carry, (out.pop(0) if ends else None)


def down_kernel(table, own_ref, other_ref, w_first, w_second, out_ref):
    for side, ref in enumerate((own_ref, other_ref)):

        @pl.when(pl.program_id(0) == side)
        def _():
            out_ref[0] = sum(
                lax.dot_general(
                    ref[k], w[0], (((1,), (1,)), ((), ())), preferred_element_type=f32
                )
                for k, w in enumerate((w_first, w_second))
            ).astype(bf16)


def down(unit, table, own, other, w_down):
    _, rows, _ = own.shape
    whole = pl.BlockSpec(own.shape, lambda g, t: (0, 0, 0))
    w_shape = (1,) + w_down.shape[1:]
    return pl.pallas_call(
        down_kernel,
        out_shape=jax.ShapeDtypeStruct((2, rows, w_down.shape[1]), bf16),
        grid_spec=pltpu.PrefetchScalarGridSpec(
            num_scalar_prefetch=1,
            grid=(2,),
            in_specs=[
                whole,
                whole,
                pl.BlockSpec(w_shape, lambda g, t: (t[0, 2 * unit + g], 0, 0)),
                pl.BlockSpec(w_shape, lambda g, t: (t[1, 2 * unit + g], 0, 0)),
            ],
            out_specs=pl.BlockSpec(
                (1, rows, w_down.shape[1]), lambda g, t: (t[2, 2 * unit + g], 0, 0)
            ),
        ),
    )(table, own, other, w_down, w_down)


def per_device(
    x_in,
    z_gate,
    b_proj,
    c_proj,
    dt_raw,
    a_log,
    d_skip,
    out_proj,
    residual,
    norm_gain,
    router,
    w_gate,
    w_up,
    w_down,
    block_experts,
):
    ctx, exp = lax.axis_size("ctx"), lax.axis_size("exp")
    place, column = lax.axis_index("ctx"), lax.axis_index("exp")
    chip, core = place // CORES, place % CORES
    chips = ctx // CORES
    slab_rows = x_in.shape[0]
    head_count = dt_raw.shape[0]
    head_size = x_in.shape[1] // head_count
    blocks = block_experts.shape[0]
    half_blocks = blocks // 2
    model_width = residual.shape[1]
    width = model_width // ctx
    share = model_width // exp
    sub = slab_rows // exp
    expert_count = router.shape[1]
    chunks = 2 * half_blocks
    steps = chunks + LAG * (chips - 1)

    def chunks_of(which, shift):
        raw = jnp.arange(steps + 1) - shift - LAG * jnp.where(which == 0, chips - 1 - chip, chip)
        wanted = (raw >= 0) & (raw < chunks)
        raw = jnp.clip(raw, 0, chunks - 1)
        block = raw // 2 + which * half_blocks
        return jnp.where(raw % 2 == 0, block_experts[block, 0], block_experts[block, 1]), block, wanted

    ahead_expert, ahead_block, ahead_wanted = chunks_of(1 - core, 0)
    own_expert, own_block, own_wanted = chunks_of(core, 1)
    ends_here = chip == jnp.where(core == 0, 0, chips - 1)
    table = jnp.stack(
        [
            ahead_expert,
            own_expert,
            ahead_block,
            own_block,
            ahead_wanted.astype(jnp.int32),
            own_wanted.astype(jnp.int32),
            jnp.broadcast_to(column, (steps + 1,)),
            jnp.broadcast_to(ends_here.astype(jnp.int32), (steps + 1,)),
        ],
        1,
    ).astype(jnp.int32)
    side = (core + jnp.arange(2)[None, :]) % 2
    down_blocks = (jnp.arange(half_blocks)[:, None] + side * half_blocks).reshape(-1)
    down_table = jnp.stack(
        [
            block_experts[down_blocks, 0],
            block_experts[down_blocks, 1],
            jnp.broadcast_to(side, (half_blocks, 2)).reshape(-1),
        ]
    ).astype(jnp.int32)

    head_rates = jnp.exp(a_log)
    steps_f = jax.nn.softplus(dt_raw)
    inputs_f = x_in.astype(f32).reshape(slab_rows, head_count, head_size)
    keys_f = b_proj.astype(f32)
    queries_f = c_proj.astype(f32)
    inside, own_state, entry_scale, block_decay = block_terms(
        inputs_f, steps_f, keys_f, queries_f, head_rates
    )
    entering = entering_state(own_state, block_decay, ctx, core, chip)
    from_before = entry_scale.T[..., None] * jnp.einsum(
        "ln,hpn->lhp", queries_f, entering, precision=highest
    )
    outputs = inside + from_before + d_skip[None, :, None] * inputs_f
    gated_rows = (outputs.reshape(slab_rows, -1) * jax.nn.silu(z_gate.astype(f32))).astype(bf16)
    group_term = jnp.dot(gated_rows, out_proj, preferred_element_type=f32).astype(bf16)

    def across(pieces, m):
        return lax.ppermute(
            lax.dynamic_index_in_dim(pieces, column ^ m, 0, False),
            "exp",
            [(j, j ^ m) for j in range(exp)],
        )

    by_rows = group_term.reshape(exp, sub, model_width)
    mixed = lax.dynamic_index_in_dim(by_rows, column, 0, False).astype(f32)
    for m in range(1, exp):
        mixed = mixed + across(by_rows, m).astype(f32)
    own_residual = lax.dynamic_slice_in_dim(residual, column * sub, sub, 0)
    stream = mixed + own_residual.astype(f32)
    mean_square = jnp.mean(stream * stream, axis=1, keepdims=True)
    normed = (stream * lax.rsqrt(mean_square + epsilon) * norm_gain).astype(bf16)
    logits = jnp.dot(normed, router, preferred_element_type=f32)
    named_here = lax.dynamic_index_in_dim(block_experts, place, 0, False)
    one_hot = (named_here[:, None] == jnp.arange(expert_count, dtype=jnp.int32)[None, :]).astype(f32)
    chosen = jnp.einsum("te,se->st", logits, one_hot, precision=highest)
    gates = jax.nn.sigmoid(chosen - chosen[::-1])
    gates_high = gates.astype(bf16)
    gates_low = (gates - gates_high.astype(f32)).astype(bf16)
    gate_rows = jnp.concatenate([gates_high, gates_low], 0)

    stream_rows = stream.astype(bf16).reshape(sub, exp, share).transpose(1, 0, 2)
    stream_out = jnp.zeros((exp, sub, share), bf16)
    stream_out = lax.dynamic_update_index_in_dim(
        stream_out, lax.dynamic_index_in_dim(stream_rows, column, 0, False), column, 0
    )
    for m in range(1, exp):
        stream_out = lax.dynamic_update_index_in_dim(
            stream_out, across(stream_rows, m), column ^ m, 0
        )
    stream_out = stream_out.reshape(slab_rows, share)

    extra = jnp.pad(gate_rows, ((0, 12), (0, width - sub)))
    pieces = jnp.concatenate(
        [
            normed.reshape(sub, ctx, width).transpose(1, 0, 2),
            jnp.broadcast_to(extra[None], (ctx, 16, width)),
        ],
        1,
    )
    slabs = lax.all_to_all(pieces, "ctx", split_axis=0, concat_axis=0, tiled=True)
    normed_part = slabs[:, :sub]
    gate_part = slabs[:, sub : sub + 4, :sub].astype(f32)
    gate_part = (gate_part[:, :2] + gate_part[:, 2:]).astype(bf16)
    flat = jnp.concatenate(
        [
            normed_part.reshape(ctx * sub, width),
            jnp.pad(gate_part.reshape(ctx * 2, sub), ((0, (-2 * ctx) % 16), (0, width - sub))),
        ],
        0,
    )
    received = [flat] + [
        lax.ppermute(flat, "exp", [(j, j ^ m) for j in range(exp)]) for m in range(1, exp)
    ]
    everyone = jnp.concatenate(received, 0).reshape(exp, -1, width)
    rows = everyone[:, : ctx * sub].reshape(exp, ctx, sub, width)
    all_gates = everyone[:, ctx * sub : ctx * sub + 2 * ctx, :sub].reshape(exp, ctx, 2, sub)
    all_gates = jnp.take(all_gates, column ^ jnp.arange(exp), axis=0)
    half_gates = lax.dynamic_slice_in_dim(all_gates, core * half_blocks, half_blocks, 1)
    end_gates = half_gates.transpose(1, 2, 0, 3).reshape(chunks, slab_rows, 1).astype(f32)

    def hop(a, step):
        pairs = []
        for u in range(chips - 1):
            if 0 <= step - LAG * u < chunks:
                z = chips - 1 - u
                pairs.append((z * CORES, (z - 1) * CORES))
                pairs.append((u * CORES + 1, (u + 1) * CORES + 1))
        if not pairs:
            return None
        return lax.ppermute(a, "ctx", pairs)

    def spread(a, u):
        z = chips - 1 - u
        pairs = [(u * CORES, (u + 1) * CORES), (z * CORES + 1, (z - 1) * CORES + 1)]
        return lax.ppermute(a, "ctx", pairs)

    ahead, _, _ = step_products(-1, steps, chips, table, rows, w_gate, w_up, None, None, None)
    arrived = {}
    finals = []
    reached = []
    outs = []
    distance = jnp.where(core == 0, chip, chips - 1 - chip)
    for step in range(steps):
        other = swap_cores(ahead, ctx)
        came = arrived[step - LAG] if step >= LAG else None
        ahead, carry, hidden = step_products(
            step, steps, chips, table, rows, w_gate, w_up, other, came, end_gates
        )
        arrived[step] = hop(carry, step)
        if hidden is None:
            continue
        finals.append(hidden)
        group = groups_of(chunks).get(len(finals))
        if group is None:
            continue
        _, count = group
        own = passing = jnp.stack(finals[-count:])
        for u in range(chips - 1):
            passing = spread(passing, u)
            own = jnp.where(distance == u + 1, passing, own)
            if u % 4 == 3:
                own, passing = lax.optimization_barrier((own, passing))
        reached.append((own, swap_cores(own, ctx)))
        if sum(r[0].shape[0] for r in reached) % 2 == 0:
            own = jnp.concatenate([r[0] for r in reached])
            crossed = jnp.concatenate([r[1] for r in reached])
            for k in range(0, own.shape[0], 2):
                outs.append(down(len(outs), down_table, own[k : k + 2], crossed[k : k + 2], w_down))
            reached = []
    out_part = jnp.stack(outs, 1).reshape(blocks, slab_rows, width)

    per = blocks // exp
    grouped = out_part.reshape(exp, per, slab_rows, width)
    owned = lax.dynamic_index_in_dim(grouped, column, 0, False).astype(f32)
    for m in range(1, exp):
        owned = owned + across(grouped, m).astype(f32)
    owned = owned.astype(bf16)
    result = jnp.zeros((per, slab_rows, width), bf16)
    for r in range(per):
        pairs = []
        for i in range(ctx):
            for j in range(exp):
                pairs.append((i * exp + j, (j * per + ((i % per) ^ r)) * exp + i // per))
        piece = lax.dynamic_index_in_dim(owned, (place % per) ^ r, 0, False)
        got = lax.ppermute(piece, ("ctx", "exp"), pairs)
        result = lax.dynamic_update_index_in_dim(result, got, (place % per) ^ r, 0)
    expert_out = result.transpose(1, 0, 2).reshape(slab_rows, share)
    return (stream_out, expert_out)


def solution(mesh):
    placed = (
        P("ctx", "exp"),
        P("ctx", "exp"),
        P("ctx", None),
        P("ctx", None),
        P("exp", "ctx"),
        P("exp"),
        P("exp"),
        P("exp", None),
        P("ctx", None),
        P(),
        P(),
        P(None, "ctx", "exp"),
        P(None, "ctx", "exp"),
        P(None, "ctx", "exp"),
        P(),
    )

    return jax.shard_map(
        per_device,
        mesh=mesh,
        in_specs=placed,
        out_specs=(P("ctx", "exp"), P("ctx", "exp")),
        check_vma=False,
    )
```
